32 devices in a mesh: groups: 2 (over y), ctx: 4 (over z), wt: 2 (over x), sub: 2 (over core).
Axes of the slice: x: 2, y: 2, z: 4, core: 2. Of those that a mesh axis runs over, the one named last changes fastest.
Arguments:
- queries: bfloat16 [16, 32, 128, 576], P(('groups', 'ctx'), None, ('wt', 'sub')), parts along dimension 0, may hold values from -80 to 80
- selection: int32 [16, 4, 2], P(('groups', 'ctx')), parts along dimension 0, may hold values from -1 to 15, as said below
- latent_cache: bfloat16 [128, 64, 576], P(('groups', 'ctx')), parts along dimension 0, may hold values from -8 to 8
- value_up: bfloat16 [128, 512, 128], P(None, ('wt', 'sub')), may hold values from -1 to 1
Outputs:
- attended: bfloat16 [16, 32, 128, 128], P(('groups', 'ctx'), None, ('wt', 'sub')), parts along dimension 0
The draws below stay inside these ranges and needn't reach their ends.
There are 2 independent parts, one for each index of `groups`. The reference program is written for one: setup_inputs(seed, part) draws one part's arguments, and reference() takes and returns one part's arrays. A program takes and returns all parts, laid end to end along the dimension named above; an argument that names none is the same for every part. Nothing has to cross between parts.
Inputs may be any that keep to these rules, and one draw needn't show every extreme that they name: `selection`: entry [c, o, s] is the number of a block among the 16 of owner o, or -1 for an empty slot; in an owner's slots live entries come first and differ. Each query block has 4 live entries in all, and in every query block some owner fills all 2 slots.
All inputs are finite; a program needn't handle non-finite values.
Results may differ from the reference program's by a relative error of at most 0.008.
Values may be sent and summed in bfloat16 or wider, within the bound.
No kernel may reach another device: no remote copies, remote signals or barrier semaphores. Data moves between devices by JAX's collectives and lax.ppermute only.
A program may use at most 128 MiB of HBM per device.

```python
import jax
import jax.numpy as jnp
from jax import lax

HEADS = 128
LAT = 512
ROPE = 64
NOPE = 128
VDIM = 128
BLK = 64
QC = 32
BLK_OWN = 16
BLOCKS = 64
SPAN_ALL = 8
N_CTX = 4


def build_all(key):
    key_sel = jax.random.fold_in(key, 101)
    key_rank = jax.random.fold_in(key, 202)
    key_cache = jax.random.fold_in(key, 303)
    key_query = jax.random.fold_in(key, 404)
    rankings = jax.vmap(lambda k: jax.random.permutation(k, BLK_OWN))(jax.random.split(key_rank, N_CTX))

    def one_span(span_key):
        first, second, third, fourth = jax.random.split(span_key, 4)
        order = jax.random.permutation(first, N_CTX)
        hottest = jax.random.randint(second, (), 1, N_CTX // 4 + 1)
        position = jnp.zeros((N_CTX,), jnp.int32).at[order].set(jnp.arange(N_CTX, dtype=jnp.int32))
        loads = jnp.where(position < hottest, 2, jnp.where(position < 2 * hottest, 0, 1))
        picks = jnp.min(jax.random.randint(third, (4, N_CTX), 0, BLK_OWN), axis=0)
        jumps = jax.random.randint(fourth, (N_CTX,), 0, BLK_OWN - 1)
        owner_rows = jnp.arange(N_CTX)
        lead = rankings[owner_rows, picks]
        other = rankings[owner_rows, (picks + 1 + jumps) % BLK_OWN]
        slot_zero = jnp.where(loads >= 1, lead, -1)
        slot_one = jnp.where(loads >= 2, other, -1)
        chosen = jnp.stack([slot_zero, slot_one], axis=1).astype(jnp.int32)
        target = (order[0] * BLK_OWN + lead[order[0]]).astype(jnp.int32)
        return (chosen, target)
    selection, targets = jax.vmap(one_span)(jax.random.split(key_sel, SPAN_ALL))
    cache = jnp.clip(jax.random.normal(key_cache, (BLOCKS, BLK, LAT + ROPE), jnp.float32), -6.0, 6.0)
    query = jnp.clip(1.2 * jax.random.normal(key_query, (SPAN_ALL, QC, HEADS, LAT + ROPE), jnp.float32), -7.2, 7.2)
    return (selection, cache, query)


def draw_queries(key, part):
    selection, cache, query = build_all(key)
    return query.astype(jnp.bfloat16)


def draw_selection(key, part):
    selection, cache, query = build_all(key)
    return selection


def draw_latent_cache(key, part):
    selection, cache, query = build_all(key)
    return cache.astype(jnp.bfloat16)


def block_levels(stream_key, dims, shards, low, high):
    loudness, own = 1.0, jax.random.fold_in(stream_key, 6)
    for axis_at, blocks in shards:
        steps = jnp.exp(jax.random.uniform(jax.random.fold_in(own, axis_at), (blocks,), jnp.float32, low / len(shards), high / len(shards)))
        loudness = loudness * jnp.repeat(steps, dims[axis_at] // blocks).reshape([-1 if axis == axis_at else 1 for axis in range(len(dims))])
    return loudness


def noise(rng, dims, width, most, shards=(), kind=jnp.bfloat16):
    entries = width * jax.random.normal(rng, dims, jnp.float32)
    if shards:
        entries = entries * block_levels(rng, dims, shards, -0.22, 0.18)
    return jnp.clip(entries, -most, most).astype(kind)


def setup_inputs(seed: int = 0, part: int = 0) -> dict:
    seeds = jax.random.split(jax.random.key(seed), 5)
    part_splits = jax.random.split(jax.random.fold_in(seeds[4], part), 5)
    queries = draw_queries(jax.random.fold_in(jax.random.fold_in(seeds[4], part), 71), part)
    selection = draw_selection(jax.random.fold_in(jax.random.fold_in(seeds[4], part), 71), part)
    latent_cache = draw_latent_cache(jax.random.fold_in(jax.random.fold_in(seeds[4], part), 71), part)
    value_up = noise(seeds[3], (HEADS, LAT, VDIM), (LAT // 16) ** -0.5, 1.0, ((1, 4),))
    return dict(queries=queries, selection=selection, latent_cache=latent_cache, value_up=value_up)


def one_block(latent_cache, value_up, query, chosen):
    owner_base = (jnp.arange(N_CTX, dtype=jnp.int32) * BLK_OWN)[:, None]
    numbers = (owner_base + jnp.clip(chosen, 0, BLK_OWN - 1)).astype(jnp.int32)
    keys = latent_cache[numbers.reshape(-1)].reshape(-1, LAT + ROPE)
    live = jnp.repeat((chosen >= 0).reshape(-1), BLK)
    rows = query.reshape(-1, LAT + ROPE)
    scores = jnp.einsum("rd,kd->rk", rows, keys, preferred_element_type=jnp.float32)
    scores = scores * jnp.float32((NOPE + ROPE) ** -0.5)
    scores = jnp.where(live[None, :], scores, -jnp.inf)
    expo = jnp.exp(scores - jnp.max(scores, axis=1, keepdims=True))
    totals = jnp.sum(expo, axis=1, keepdims=True)
    weights = expo.astype(jnp.bfloat16)
    latent = (jnp.dot(weights, keys[:, :LAT], preferred_element_type=jnp.float32) / totals).astype(jnp.bfloat16)
    latent = latent.reshape(QC, HEADS, LAT)
    out = jnp.einsum("qhl,hlv->qhv", latent.astype(jnp.float32), value_up.astype(jnp.float32))
    return out.astype(jnp.bfloat16)


def reference(queries, selection, latent_cache, value_up):
    def step(pair):
        return one_block(latent_cache, value_up, pair[0], pair[1])
    return lax.map(step, (queries, selection))
```

```python
import functools

import jax
import jax.numpy as jnp
from jax import lax
from jax.experimental import pallas as pl
from jax.experimental.pallas import tpu as pltpu
from jax.sharding import PartitionSpec as P

LAT = 512
ROPE = 64
NOPE = 128
SCALE = (NOPE + ROPE) ** (-0.5)


SMEM = pl.BlockSpec(memory_space=pltpu.SMEM)
VMEM = pl.BlockSpec(memory_space=pltpu.VMEM)
ANY = pl.BlockSpec(memory_space=pl.ANY)


def pick_kernel(place_ref, asked_ref, cache_ref, out_ref, sem):
    owners, spans = out_ref.shape[:2]
    slots = asked_ref.shape[1] // (owners * spans)
    mine, slot = place_ref[0], place_ref[1]
    copies = []
    for owner in range(owners):
        for span in range(spans):
            number = jnp.maximum(asked_ref[mine ^ owner, (span * owners + mine) * slots + slot], 0)
            copies.append(
                pltpu.make_async_copy(cache_ref.at[number], out_ref.at[owner, span], sem)
            )
    for copy in copies:
        copy.start()
    for copy in copies:
        copy.wait()


def pick(place, asked, cache, spans):
    owners = asked.shape[0]
    return pl.pallas_call(
        pick_kernel,
        out_shape=jax.ShapeDtypeStruct((owners, spans) + cache.shape[1:], cache.dtype),
        in_specs=[SMEM, SMEM, VMEM],
        out_specs=ANY,
        scratch_shapes=[pltpu.SemaphoreType.DMA],
        name="pick",
    )(place, asked, cache)


def attend_kernel(place_ref, chosen_ref, query_ref, mine_ref, other_ref, out_ref, keys):
    spans, owners, slots = chosen_ref.shape
    block, width = mine_ref.shape[2:]
    heads, _, per_span, _ = query_ref.shape

    @pl.when(pl.program_id(0) == 0)
    def _():
        first = place_ref[1] == 0
        for span in range(spans):
            filled = jnp.int32(0)
            for owner in range(owners):
                for slot in range(slots):
                    live = chosen_ref[span, owner, slot] >= 0
                    here = first if slot == 0 else jnp.logical_not(first)
                    start = pl.multiple_of(jnp.minimum(filled, owners - 1) * block, block)

                    @pl.when(jnp.logical_and(live, here))
                    def _():
                        keys[span, pl.ds(start, block), :] = mine_ref[owner, span]

                    @pl.when(jnp.logical_and(live, jnp.logical_not(here)))
                    def _():
                        keys[span, pl.ds(start, block), :] = other_ref[owner, span]

                    filled = filled + live.astype(jnp.int32)

    for span in range(spans):
        rows = query_ref[:, span].reshape(heads * per_span, width)
        scores = lax.dot_general(
            rows, keys[span], (((1,), (1,)), ((), ())), preferred_element_type=jnp.float32
        )
        expo = jnp.exp((scores - jnp.max(scores, axis=1, keepdims=True)) * jnp.float32(SCALE))
        totals = jnp.sum(expo, axis=1, keepdims=True)
        latent = jnp.dot(
            expo.astype(jnp.bfloat16), keys[span, :, :LAT], preferred_element_type=jnp.float32
        )
        latent = latent * (1.0 / totals)
        out_ref[:, span] = latent.astype(jnp.bfloat16).reshape(heads, per_span, LAT)


def attend(place, chosen, query, mine, other):
    heads, spans, per_span, width = query.shape
    owners, block = mine.shape[0], mine.shape[2]
    group = 8
    return pl.pallas_call(
        attend_kernel,
        grid=(heads // group,),
        out_shape=jax.ShapeDtypeStruct((heads, spans, per_span, LAT), jnp.bfloat16),
        in_specs=[
            SMEM,
            SMEM,
            pl.BlockSpec((group, spans, per_span, width), lambda i: (i, 0, 0, 0)),
            VMEM,
            VMEM,
        ],
        out_specs=pl.BlockSpec((group, spans, per_span, LAT), lambda i: (i, 0, 0, 0)),
        scratch_shapes=[pltpu.VMEM((spans, owners * block, width), jnp.bfloat16)],
        name="attend",
    )(place, chosen, query, mine, other)


def project_kernel(moves, place_ref, latent_ref, *refs):
    count = len(moves)
    pieces, out_ref = refs[:count], refs[count]
    weights, summed, sem = refs[count + 1 :]
    heads, spans, per_span, _ = latent_ref.shape
    rows = pieces[0].shape[-2]
    copies = []
    for at, (take, slices) in enumerate(zip(pieces, moves)):
        for source, head_from, place_at, head_to, number in slices:
            start = place_ref[head_from] if head_from is not None else 0
            view = take.at[source] if source is not None else take
            row_at = pl.multiple_of(place_ref[place_at] * rows, rows)
            copies.append(
                pltpu.make_async_copy(
                    view.at[pl.ds(start, number)],
                    weights.at[pl.ds(head_to, number), pl.ds(row_at, rows)],
                    sem,
                )
            )
    for copy in copies:
        copy.start()
    for copy in copies:
        copy.wait()
    for head in range(heads):
        lat = latent_ref[head].reshape(spans * per_span, LAT)
        part = jnp.dot(lat, weights[head], preferred_element_type=jnp.float32)
        summed[pl.ds(head, spans * per_span, stride=heads), :] = part
    out_ref[...] = summed[...].astype(jnp.bfloat16).reshape(out_ref.shape)


def project(place, latent, pieces, moves):
    heads, spans, per_span, _ = latent.shape
    values = pieces[0].shape[-1]
    return pl.pallas_call(
        functools.partial(project_kernel, moves),
        out_shape=jax.ShapeDtypeStruct((spans, per_span, heads, values), jnp.bfloat16),
        in_specs=[SMEM, VMEM] + [ANY] * len(pieces),
        out_specs=VMEM,
        scratch_shapes=[
            pltpu.VMEM((heads, LAT, values), jnp.bfloat16),
            pltpu.VMEM((spans * per_span * heads, values), jnp.float32),
            pltpu.SemaphoreType.DMA,
        ],
        name="project",
    )(place, latent, *pieces)


def hop(array, names, sizes, move):
    total = 1
    for size in sizes:
        total *= size
    pairs = []
    for at in range(total):
        left, place = at, []
        for size in reversed(sizes):
            place.insert(0, left % size)
            left //= size
        target = move(*place)
        flat = 0
        for size, index in zip(sizes, target):
            flat = flat * size + index
        pairs.append((at, flat))
    return lax.ppermute(array, names, pairs)


def weight_pieces(value_up, heads):
    groups, wide, subs = (lax.axis_size(name) for name in ("groups", "wt", "sub"))
    group, wt, sub = (lax.axis_index(name) for name in ("groups", "wt", "sub"))
    here = wt * subs + sub
    scalars = [here * heads]
    pieces, moves = [value_up], []

    def scalar(value):
        scalars.append(value)
        return len(scalars) - 1

    moves.append([(None, 0, scalar(here), 0, heads)])
    for step in range(1, subs):
        partner = (sub + step) % subs
        data = lax.dynamic_slice_in_dim(value_up, (wt * subs + partner) * heads, heads, 0)
        pieces.append(hop(data, "sub", (subs,), lambda s: ((s + step) % subs,)))
        moves.append([(None, None, scalar(wt * subs + (sub - step) % subs), 0, heads)])
    forward = (heads * 2 // 3) if groups == 2 and subs == 2 else 0
    names = ("groups", "wt", "sub")
    sizes = (groups, wide, subs)
    for step in range(1, wide):
        far = (wt + step) % wide
        near = (wt - step) % wide
        if forward:
            same = sub ^ group
            cross = same ^ 1

            def part(core, start, count, twist):
                data = lax.dynamic_slice_in_dim(
                    value_up, (far * subs + core) * heads + start, count, 0
                )
                return hop(
                    data, names, sizes, lambda g, w, s: (g, (w + step) % wide, s ^ g ^ twist)
                )

            ahead = part(same, 0, forward, 0)
            passed = hop(ahead, "groups", (groups,), lambda g: (g ^ 1,))
            rest = heads - forward
            rest_same = part(same, forward, rest, 0)
            rest_cross = part(cross, forward, rest, 1)
            from_same = scalar(near * subs + same)
            from_cross = scalar(near * subs + cross)
            pieces += [ahead, passed, rest_same, rest_cross]
            moves += [
                [(None, None, from_same, 0, forward)],
                [(None, None, from_cross, 0, forward)],
                [(None, None, from_same, forward, rest)],
                [(None, None, from_cross, forward, rest)],
            ]
        else:
            for twist in range(subs):
                partner = (sub + twist) % subs
                data = lax.dynamic_slice_in_dim(
                    value_up, (far * subs + partner) * heads, heads, 0
                )
                pieces.append(
                    hop(
                        data,
                        names,
                        sizes,
                        lambda g, w, s: (g, (w + step) % wide, (s + twist) % subs),
                    )
                )
                moves.append(
                    [(None, None, scalar(near * subs + (sub - twist) % subs), 0, heads)]
                )
    return pieces, moves, jnp.stack(scalars).astype(jnp.int32)


def per_device(queries, selection, latent_cache, value_up):
    owners = lax.axis_size("ctx")
    spans, per_span, heads, width = queries.shape
    place = jnp.stack([lax.axis_index("ctx"), lax.axis_index("sub")]).astype(jnp.int32)

    pieces, moves, scalars = weight_pieces(value_up, heads)

    asked = selection.reshape(1, -1)
    step = 1
    while step < owners:
        got = hop(asked, "ctx", (owners,), lambda c: (c ^ step,))
        asked = jnp.concatenate([asked, got])
        step *= 2
    picked = pick(place, asked, latent_cache, spans)
    mine = lax.all_to_all(picked, "ctx", split_axis=0, concat_axis=0, tiled=True)
    other = hop(mine, "sub", (lax.axis_size("sub"),), lambda s: (s ^ 1,))
    query = jnp.transpose(queries, (2, 0, 1, 3))
    latent = attend(place, selection, query, mine, other)
    return project(scalars, latent, pieces, moves)


def solution(mesh):
    placed = (
        P(("groups", "ctx"), None, ("wt", "sub"), None),
        P(("groups", "ctx"), None, None),
        P(("groups", "ctx"), None, None),
        P(None, ("wt", "sub"), None),
    )
    return jax.shard_map(
        per_device,
        mesh=mesh,
        in_specs=placed,
        out_specs=P(("groups", "ctx"), None, ("wt", "sub"), None),
        check_vma=False,
    )
```

```python
import jax
import jax.numpy as jnp
from jax import lax
from jax.experimental import pallas as pl
from jax.experimental.pallas import tpu as pltpu
from jax.sharding import PartitionSpec as P

LAT = 512
ROPE = 64
NOPE = 128
SCALE = (NOPE + ROPE) ** (-0.5)
AXES = ("groups", "ctx", "wt", "sub")


SMEM = pl.BlockSpec(memory_space=pltpu.SMEM)
VMEM = pl.BlockSpec(memory_space=pltpu.VMEM)
ANY = pl.BlockSpec(memory_space=pl.ANY)
HBM = pl.BlockSpec(memory_space=pltpu.HBM)


def hop(array, move, **names):
    axes = tuple(name for name in AXES if name in names)
    sizes = [names[name] for name in axes]
    total = 1
    for size in sizes:
        total *= size
    pairs = []
    for at in range(total):
        left, place = at, []
        for size in reversed(sizes):
            place.insert(0, left % size)
            left //= size
        flat = 0
        for size, index in zip(sizes, move(*place)):
            flat = flat * size + index
        pairs.append((at, flat))
    return lax.ppermute(array, axes, pairs)


def pick(asked, cache, spans, owners, mixed):
    steps = len(asked)

    def kernel(*refs):
        asked_refs, cache_ref, out_refs, sem = refs[:steps], refs[steps], refs[steps + 1 : -1], refs[-1]
        mine, slot = lax.axis_index("ctx"), lax.axis_index("sub")
        copies = []
        for entry in range(owners):
            away = entry if mixed else None
            for span in range(spans):
                if mixed:
                    which = away.bit_length()
                    at = away - (1 << (which - 1)) if which else 0
                    number = asked_refs[which][at * spans + span, slot, mine]
                    target = out_refs[entry].at[span]
                else:
                    number = asked_refs[0][entry * spans + span, slot, mine]
                    target = out_refs[0].at[entry, span]
                copies.append(
                    pltpu.make_async_copy(cache_ref.at[jnp.maximum(number, 0)], target, sem)
                )
        for copy in copies:
            copy.start()
        for copy in copies:
            copy.wait()

    block = cache.shape[1:]
    if mixed:
        shapes = [jax.ShapeDtypeStruct((spans,) + block, cache.dtype)] * owners
    else:
        shapes = [jax.ShapeDtypeStruct((owners, spans) + block, cache.dtype)]
    return pl.pallas_call(
        kernel,
        out_shape=shapes,
        in_specs=[SMEM] * steps + [ANY],
        out_specs=[VMEM] * len(shapes),
        scratch_shapes=[pltpu.SemaphoreType.DMA],
        compiler_params=pltpu.CompilerParams(vmem_limit_bytes=16 << 20),
        name="pick",
    )(*asked, cache)


def weight_pieces(value_up, heads):
    groups, ctx, wide, subs = (lax.axis_size(name) for name in AXES)
    group, at, wt, sub = (lax.axis_index(name) for name in AXES)
    pieces, rules = [value_up], [lambda g, c, w, s: ((w * subs + s) * heads, w * subs + s, 0, heads)]

    def cut(chip, core, start, count):
        return lax.dynamic_slice_in_dim(value_up, (chip * subs + core) * heads + start, count, 0)

    square = groups == 2 and subs == 2 and ctx % 2 == 0
    half = heads // 2
    for step in range(1, wide):
        far = (wt + step) % wide
        sizes = dict(groups=groups, wt=wide, sub=subs)
        if square:
            first = hop(
                cut(far, sub ^ group, at % 2 * half, half),
                lambda g, w, s: (g, (w + step) % wide, s ^ g),
                **sizes,
            )
            last = hop(
                cut(far, sub ^ group ^ 1, (1 - at % 2) * half, half),
                lambda g, w, s: (g, (w + step) % wide, s ^ g ^ 1),
                **sizes,
            )
            side = hop(first, lambda g: (g ^ 1,), groups=groups)
            over = hop(first, lambda c: (c ^ 1,), ctx=ctx)
            for piece, across, along in ((first, 0, 0), (side, 1, 0), (over, 0, 1), (last, 1, 1)):
                pieces.append(piece)
                rules.append(
                    lambda g, c, w, s, step=step, across=across, along=along: (
                        0,
                        (w - step) % wide * subs + (s ^ g ^ across),
                        (c % 2 ^ along) * half,
                        half,
                    )
                )
        else:
            for twist in range(subs):
                piece = hop(
                    cut(far, (sub + twist) % subs, 0, heads),
                    lambda g, w, s: (g, (w + step) % wide, (s + twist) % subs),
                    **sizes,
                )
                pieces.append(piece)
                rules.append(
                    lambda g, c, w, s, step=step, twist=twist: (
                        0,
                        (w - step) % wide * subs + (s - twist) % subs,
                        0,
                        heads,
                    )
                )
    for step in range(1, subs):
        pieces.append(
            hop(cut(wt, (sub + step) % subs, 0, heads), lambda s: ((s + step) % subs,), sub=subs)
        )
        rules.append(
            lambda g, c, w, s, step=step: (0, w * subs + (s - step) % subs, 0, heads)
        )
    return pieces, rules


def attend(selection, query, mine, other, pieces, rules, mixed):
    heads, spans, per_span, width = query.shape
    slots, owners = selection.shape[1:]
    block = mine[0].shape[-2]
    rows, values = pieces[0].shape[1:]
    tokens = spans * per_span
    chunks = 2
    group = heads // chunks
    parts, landed = len(pieces), len(mine)

    def kernel(chosen_ref, query_ref, *refs):
        mine_refs, other_refs = refs[:landed], refs[landed : 2 * landed]
        piece_refs, out_ref = refs[2 * landed : 2 * landed + parts], refs[2 * landed + parts]
        keys, latent, weights, summed, result, weight_sem, out_sem = refs[2 * landed + parts + 1 :]
        place = [lax.axis_index(name) for name in AXES]
        arrivals = []
        for piece, rule in zip(piece_refs, rules):
            head_from, number, head_to, count = rule(*place)
            row_at = pl.multiple_of(number * rows, rows)
            arrivals.append(
                pltpu.make_async_copy(
                    piece.at[pl.ds(head_from, count)],
                    weights.at[pl.ds(head_to, count), pl.ds(row_at, rows)],
                    weight_sem,
                )
            )
        for copy in arrivals:
            copy.start()

        at, sub = place[1], place[3]
        for span in range(spans):
            filled = jnp.int32(0)
            for entry in range(owners):
                owner = at ^ entry if mixed else entry
                if mixed:
                    own, across = mine_refs[entry].at[span], other_refs[entry].at[span]
                else:
                    own, across = mine_refs[0].at[entry, span], other_refs[0].at[entry, span]
                for slot in range(slots):
                    live = chosen_ref[span, slot, owner] >= 0
                    here = sub == slot
                    start = pl.multiple_of(jnp.minimum(filled, owners - 1) * block, block)

                    @pl.when(jnp.logical_and(live, here))
                    def _():
                        keys[span, pl.ds(start, block), :] = own[...]

                    @pl.when(jnp.logical_and(live, jnp.logical_not(here)))
                    def _():
                        keys[span, pl.ds(start, block), :] = across[...]

                    filled = filled + live.astype(jnp.int32)

        def score(step):
            span, first = step % spans, step // spans * group
            lines = query_ref[first : first + group, span].reshape(group * per_span, width)
            return lax.dot_general(
                lines, keys[span], (((1,), (1,)), ((), ())), preferred_element_type=jnp.float32
            )

        def soften(scores):
            top = jnp.max(scores, axis=1, keepdims=True)
            expo = jnp.exp((scores - top) * jnp.float32(SCALE))
            return expo.astype(jnp.bfloat16), 1.0 / jnp.sum(expo, axis=1, keepdims=True)

        def gather(step, expo, inverse):
            span, first = step % spans, step // spans * group
            mixed_rows = jnp.dot(expo, keys[span, :, :LAT], preferred_element_type=jnp.float32)
            latent[first : first + group, span] = (
                (mixed_rows * inverse).astype(jnp.bfloat16).reshape(group, per_span, LAT)
            )

        steps = chunks * spans
        scores = {step: score(step) for step in range(min(2, steps))}
        soft = {0: soften(scores.pop(0))}
        for step in range(steps):
            if step + 2 < steps:
                scores[step + 2] = score(step + 2)
            if step + 1 < steps:
                soft[step + 1] = soften(scores.pop(step + 1))
            gather(step, *soft.pop(step))

        for copy in arrivals:
            copy.wait()
        departures = []
        for first in range(0, heads, 16):
            for head in range(first, first + 16):
                lines = latent[head].reshape(tokens, LAT)
                summed[pl.ds(head, tokens, stride=heads), :] = jnp.dot(
                    lines, weights[head], preferred_element_type=jnp.float32
                )
            whole = summed[...].reshape(tokens, heads, values)[:, first : first + 16]
            result[:, :, first : first + 16] = whole.astype(jnp.bfloat16).reshape(
                spans, per_span, 16, values
            )
            departures.append(
                pltpu.make_async_copy(
                    result.at[:, :, pl.ds(first, 16)], out_ref.at[:, :, pl.ds(first, 16)], out_sem
                )
            )
            departures[-1].start()
        for copy in departures:
            copy.wait()

    return pl.pallas_call(
        kernel,
        out_shape=jax.ShapeDtypeStruct((spans, per_span, heads, values), jnp.bfloat16),
        in_specs=[SMEM] + [VMEM] * (1 + 2 * landed) + [HBM] + [ANY] * (parts - 1),
        out_specs=ANY,
        scratch_shapes=[
            pltpu.VMEM((spans, owners * block, width), jnp.bfloat16),
            pltpu.VMEM((heads, spans, per_span, LAT), jnp.bfloat16),
            pltpu.VMEM((heads, LAT, values), jnp.bfloat16),
            pltpu.VMEM((tokens * heads, values), jnp.float32),
            pltpu.VMEM((spans, per_span, heads, values), jnp.bfloat16),
            pltpu.SemaphoreType.DMA,
            pltpu.SemaphoreType.DMA,
        ],
        compiler_params=pltpu.CompilerParams(vmem_limit_bytes=(24 if mixed else 44) << 20),
        name="attend",
    )(selection, query, *mine, *other, *pieces)


def per_device(queries, selection, latent_cache, value_up):
    owners, subs = lax.axis_size("ctx"), lax.axis_size("sub")
    spans, _, heads, _ = queries.shape
    chosen = jnp.transpose(selection, (0, 2, 1))
    mixed = owners <= 8

    asked = [chosen]
    while (1 << (len(asked) - 1)) < owners:
        step = 1 << (len(asked) - 1)
        whole = jnp.concatenate(asked) if len(asked) > 1 else chosen
        asked.append(hop(whole, lambda c: (c ^ step,), ctx=owners))
    if not mixed:
        order = jnp.arange(owners) ^ lax.axis_index("ctx")
        whole = jnp.concatenate(asked).reshape((owners,) + chosen.shape)[order]
        asked = [whole.reshape((owners * spans,) + chosen.shape[1:])]
    picked = pick(asked, latent_cache, spans, owners, mixed)
    if mixed:
        mine = [None] * owners
        for entry in sorted(range(owners), key=lambda e: (e == 0, e == 1, e)):
            got = picked[entry]
            if entry:
                got = hop(got, lambda c: (c ^ entry,), ctx=owners)
            mine[entry] = got
    else:
        mine = [lax.all_to_all(picked[0], "ctx", split_axis=0, concat_axis=0, tiled=True)]
    other = []
    for entry, piece in enumerate(mine):
        other.append(hop(piece, lambda s: (s ^ 1,), sub=subs))
    pieces, rules = weight_pieces(value_up, heads)
    query = jnp.transpose(queries, (2, 0, 1, 3))
    return attend(chosen, query, mine, other, pieces, rules, mixed)


def solution(mesh):
    placed = (
        P(("groups", "ctx"), None, ("wt", "sub"), None),
        P(("groups", "ctx"), None, None),
        P(("groups", "ctx"), None, None),
        P(None, ("wt", "sub"), None),
    )

    return jax.shard_map(
        per_device,
        mesh=mesh,
        in_specs=placed,
        out_specs=P(("groups", "ctx"), None, ("wt", "sub"), None),
        check_vma=False,
    )
```

```python
import jax
import jax.numpy as jnp
from jax import lax
from jax.experimental import pallas as pl
from jax.experimental.pallas import tpu as pltpu
from jax.sharding import PartitionSpec as P

LAT = 512
ROPE = 64
NOPE = 128
SCALE = (NOPE + ROPE) ** (-0.5)
AXES = ("groups", "ctx", "wt", "sub")
PARTS = (9, 11)


SMEM = pl.BlockSpec(memory_space=pltpu.SMEM)
VMEM = pl.BlockSpec(memory_space=pltpu.VMEM)
ANY = pl.BlockSpec(memory_space=pl.ANY)
HBM = pl.BlockSpec(memory_space=pltpu.HBM)


def hop(array, move, **names):
    axes = tuple(name for name in AXES if name in names)
    sizes = [names[name] for name in axes]
    total = 1
    for size in sizes:
        total *= size
    pairs = []
    for at in range(total):
        left, place = at, []
        for size in reversed(sizes):
            place.insert(0, left % size)
            left //= size
        flat = 0
        for size, index in zip(sizes, move(*place)):
            flat = flat * size + index
        pairs.append((at, flat))
    return lax.ppermute(array, axes, pairs)


def pick(asked, cache, spans):
    parts = len(asked)
    block, width = cache.shape[1:]
    whole = asked[0].shape[0] > spans

    def kernel(*refs):
        asked_refs, cache_ref, out_refs = refs[:parts], refs[parts], refs[parts + 1 :]
        mine, slot = lax.axis_index("ctx"), lax.axis_index("sub")
        for part in range(parts):
            for first in range(0, asked[part].shape[0], spans):
                out = out_refs[0].at[first // spans] if whole else out_refs[part]
                tails = []
                for span in range(spans):
                    number = jnp.maximum(asked_refs[part][first + span, slot, mine], 0)
                    out[:, span * LAT : (span + 1) * LAT] = cache_ref[number, :, :LAT]
                    tails.append(cache_ref[number, :, LAT:])
                out[:, spans * LAT :] = jnp.concatenate(tails, axis=1)

    shape = (block, spans * width)
    if whole:
        shapes = [jax.ShapeDtypeStruct((asked[0].shape[0] // spans,) + shape, cache.dtype)]
    else:
        shapes = [jax.ShapeDtypeStruct(shape, cache.dtype)] * parts
    return pl.pallas_call(
        kernel,
        out_shape=shapes,
        in_specs=[SMEM] * parts + [VMEM],
        out_specs=[VMEM] * len(shapes),
        compiler_params=pltpu.CompilerParams(vmem_limit_bytes=16 << 20),
        name="pick",
    )(*asked, cache)


def cut(value_up, wanted):
    count = sum(len(runs) for runs in wanted)

    def kernel(whole_ref, *refs):
        outs, sems = refs[:-1], refs[-1]
        place = [lax.axis_index(name) for name in AXES]
        copies = []
        for runs, out in zip(wanted, outs):
            at = 0
            for first, heads in runs:
                copies.append(
                    pltpu.make_async_copy(
                        whole_ref.at[pl.ds(first(*place), heads)],
                        out.at[pl.ds(at, heads)],
                        sems.at[len(copies)],
                    )
                )
                at += heads
        for copy in copies:
            copy.start()
        for copy in copies:
            copy.wait()

    return pl.pallas_call(
        kernel,
        out_shape=[
            jax.ShapeDtypeStruct(
                (sum(heads for _, heads in runs),) + value_up.shape[1:], value_up.dtype
            )
            for runs in wanted
        ],
        in_specs=[HBM],
        out_specs=[VMEM] * len(wanted),
        scratch_shapes=[pltpu.SemaphoreType.DMA((count,))],
        compiler_params=pltpu.CompilerParams(vmem_limit_bytes=16 << 20),
        name="cut",
    )(pltpu.with_memory_space_constraint(value_up, pltpu.HBM))


def weight_pieces(value_up, heads, query):
    groups, ctx, wide, subs = (lax.axis_size(name) for name in AXES)
    pieces = [value_up]
    rules = [lambda g, c, w, s: [((w * subs + s) * heads, w * subs + s, 0, heads)]]
    square = groups == 2 and subs == 2 and ctx % 2 == 0
    one, two = heads * PARTS[0] // 32, heads * PARTS[1] // 32
    last = 2 * one + two
    rest = heads - last
    sizes = dict(groups=groups, wt=wide, sub=subs)
    wanted, labels, moves = [], [], []

    def want(label, step, core, runs, move):
        def first_of(start):
            return lambda g, c, w, s: ((w + step) % wide * subs + core(g, s)) * heads + start(c)

        wanted.append([(first_of(start), count) for start, count in runs])
        labels.append(label)
        moves.append(move)

    for step in range(1, wide):
        if square:
            same = lambda g, w, s, step=step: (g, (w + step) % wide, s ^ g)
            cross = lambda g, w, s, step=step: (g, (w + step) % wide, s ^ g ^ 1)
            here, there = lambda g, s: s ^ g, lambda g, s: s ^ g ^ 1
            want("wone", step, here, [(lambda c: c % 2 * one, one)], same)
            want("wtwo", step, here, [(lambda c: 2 * one, two)], same)
            want("wsame", step, here, [(lambda c: last, rest)], same)
            want(
                "wcross",
                step,
                there,
                [(lambda c: (1 - c % 2) * one, one), (lambda c: last, rest)],
                cross,
            )
        else:
            for twist in range(subs):
                move = lambda g, w, s, step=step, twist=twist: (
                    g,
                    (w + step) % wide,
                    (s + twist) % subs,
                )
                there = lambda g, s, twist=twist: (s + twist) % subs
                want("wfar", step, there, [(lambda c: 0, heads)], move)
    for step in range(1, subs):
        there = lambda g, s, step=step: (s + step) % subs
        move = lambda g, w, s, step=step: (g, w, (s + step) % subs)
        want("wcore", 0, there, [(lambda c: 0, heads)], move)
    got = [None] * len(wanted)
    ahead = [at for at, label in enumerate(labels) if label == "wone"]
    for chosen in (ahead, [at for at in range(len(labels)) if at not in ahead]):
        if not chosen:
            continue
        found = cut(value_up, [wanted[at] for at in chosen])
        for at, piece in zip(chosen, found):
            got[at] = hop(piece, moves[at], **sizes)

    def add(piece, step, core, runs):
        pieces.append(piece)

        def rule(g, c, w, s):
            at, found = 0, []
            for start, count in runs:
                found.append((at, (w - step) % wide * subs + core(g, s), start(c), count))
                at += count
            return found

        rules.append(rule)

    at = 0
    for step in range(1, wide):
        if square:
            first, second, direct, crossed = got[at : at + 4]
            at += 4
            swap = lambda g: (g ^ 1,)
            side_first = hop(first, swap, groups=groups)
            over = hop(first, lambda c: (c ^ 1,), ctx=ctx)
            second, query = lax.optimization_barrier((second, query))
            side_second = hop(second, swap, groups=groups)
            here, there = lambda g, s: s ^ g, lambda g, s: s ^ g ^ 1
            own, next_to = lambda c: c % 2 * one, lambda c: (1 - c % 2) * one
            add(first, step, here, [(own, one)])
            add(over, step, here, [(next_to, one)])
            add(second, step, here, [(lambda c: 2 * one, two)])
            add(direct, step, here, [(lambda c: last, rest)])
            add(side_first, step, there, [(own, one)])
            add(side_second, step, there, [(lambda c: 2 * one, two)])
            add(crossed, step, there, [(next_to, one), (lambda c: last, rest)])
        else:
            for twist in range(subs):
                there = lambda g, s, twist=twist: (s - twist) % subs
                add(got[at], step, there, [(lambda c: 0, heads)])
                at += 1
    for step in range(1, subs):
        add(got[at], 0, lambda g, s, step=step: (s - step) % subs, [(lambda c: 0, heads)])
        at += 1
    return pieces, rules, query, 2 * one if square else 0


def attend(selection, query, mine, other, mixed):
    spans, heads, per_span, width = query.shape
    _, slots, owners = selection.shape
    block = mine[0].shape[-2]
    rotary = width - LAT
    chunks = 2
    group = heads // chunks
    landed = len(mine)

    def kernel(chosen_ref, query_ref, *refs):
        mine_refs, other_refs = refs[:landed], refs[landed : 2 * landed]
        latent, keys = refs[2 * landed :]
        at, sub = lax.axis_index("ctx"), lax.axis_index("sub")
        for span in range(spans):
            filled = jnp.int32(0)
            latent_at = slice(span * LAT, (span + 1) * LAT)
            for entry in range(owners):
                owner = at ^ entry if mixed else entry
                own = mine_refs[entry] if mixed else mine_refs[0].at[entry]
                across = other_refs[entry] if mixed else other_refs[0].at[entry]
                for slot in range(slots):
                    live = chosen_ref[span, slot, owner] >= 0
                    here = sub == slot
                    start = pl.multiple_of(jnp.minimum(filled, owners - 1) * block, block)

                    @pl.when(live)
                    def _():
                        keys[span, pl.ds(start, block), :LAT] = jnp.where(
                            here, own[:, latent_at], across[:, latent_at]
                        )
                        keys[span, pl.ds(start, block), LAT:] = jnp.where(
                            here, own[:, spans * LAT :], across[:, spans * LAT :]
                        )

                    filled = filled + live.astype(jnp.int32)
            if span:
                at_span = LAT + span * rotary
                keys[span, :, LAT:width] = keys[span, :, at_span : at_span + rotary]

        def score(step):
            span, first = step % spans, step // spans * group
            lines = query_ref[span, first : first + group].reshape(group * per_span, width)
            return lax.dot_general(
                lines,
                keys[span, :, :width],
                (((1,), (1,)), ((), ())),
                preferred_element_type=jnp.float32,
            )

        def soften(scores):
            top = jnp.max(scores, axis=1, keepdims=True)
            expo = jnp.exp((scores - top) * jnp.float32(SCALE))
            return expo.astype(jnp.bfloat16), 1.0 / jnp.sum(expo, axis=1, keepdims=True)

        def gather(step, expo, inverse):
            span, first = step % spans, step // spans * group
            mixed_rows = jnp.dot(expo, keys[span, :, :LAT], preferred_element_type=jnp.float32)
            latent[first : first + group, span] = (
                (mixed_rows * inverse).astype(jnp.bfloat16).reshape(group, per_span, LAT)
            )

        steps = chunks * spans
        scores = {step: score(step) for step in range(min(2, steps))}
        soft = {0: soften(scores.pop(0))}
        for step in range(steps):
            if step + 2 < steps:
                scores[step + 2] = score(step + 2)
            if step + 1 < steps:
                soft[step + 1] = soften(scores.pop(step + 1))
            gather(step, *soft.pop(step))

    return pl.pallas_call(
        kernel,
        out_shape=jax.ShapeDtypeStruct((heads, spans, per_span, LAT), jnp.bfloat16),
        in_specs=[SMEM] + [VMEM] * (1 + 2 * landed),
        out_specs=VMEM,
        scratch_shapes=[pltpu.VMEM((spans, owners * block, LAT + spans * rotary), jnp.bfloat16)],
        compiler_params=pltpu.CompilerParams(vmem_limit_bytes=(16 if mixed else 44) << 20),
        name="attend",
    )(selection, query, *mine, *other)


def project(latent, pieces, rules, split):
    heads, spans, per_span, _ = latent.shape
    rows, values = pieces[0].shape[1:]
    tokens = spans * per_span
    parts = len(pieces)
    pitch = heads + 8

    def kernel(latent_ref, *refs):
        piece_refs = refs[:parts]
        out_ref, weights, summed, result, weight_sems, out_sem = refs[parts:]
        place = [lax.axis_index(name) for name in AXES]
        arrivals = [[], []]

        def bring(group, piece, head_from, number, head_to, count):
            row_at = pl.multiple_of(number * rows, rows)
            arrivals[group].append(
                pltpu.make_async_copy(
                    piece.at[pl.ds(head_from, count)],
                    weights.at[pl.ds(head_to, count), pl.ds(row_at, rows)],
                    weight_sems.at[group],
                )
            )

        for piece, rule in zip(piece_refs, rules):
            for head_from, number, head_to, count in rule(*place):
                if not isinstance(head_to, int) or head_to + count <= split:
                    bring(1, piece, head_from, number, head_to, count)
                elif head_to >= split:
                    bring(0, piece, head_from, number, head_to, count)
                else:
                    low = split - head_to
                    bring(0, piece, head_from + low, number, split, count - low)
                    bring(1, piece, head_from, number, head_to, low)
        for group in arrivals:
            for copy in group:
                copy.start()

        departures = []
        done = set()
        for position, head in enumerate(list(range(split, heads)) + list(range(split - 1, -1, -1))):
            if position in (0, heads - split):
                for copy in arrivals[0 if position == 0 and split < heads else 1]:
                    copy.wait()
            summed[pl.ds(head, tokens, stride=pitch), :] = jnp.dot(
                latent_ref[head].reshape(tokens, LAT),
                weights[head],
                preferred_element_type=jnp.float32,
            )
            done.add(head)
            first = head // 16 * 16
            if not done.issuperset(range(first, first + 16)):
                continue
            for token in range(tokens):
                line = summed[token * pitch + first : token * pitch + first + 16, :]
                result[token // per_span, token % per_span, first : first + 16] = line.astype(
                    jnp.bfloat16
                )
            departures.append(
                pltpu.make_async_copy(
                    result.at[:, :, pl.ds(first, 16)], out_ref.at[:, :, pl.ds(first, 16)], out_sem
                )
            )
            departures[-1].start()
        for copy in departures:
            copy.wait()

    return pl.pallas_call(
        kernel,
        out_shape=jax.ShapeDtypeStruct((spans, per_span, heads, values), jnp.bfloat16),
        in_specs=[VMEM, HBM] + [ANY] * (parts - 1),
        out_specs=ANY,
        scratch_shapes=[
            pltpu.VMEM((heads, LAT, values), jnp.bfloat16),
            pltpu.VMEM((tokens * pitch, values), jnp.float32),
            pltpu.VMEM((spans, per_span, heads, values), jnp.bfloat16),
            pltpu.SemaphoreType.DMA((2,)),
            pltpu.SemaphoreType.DMA,
        ],
        compiler_params=pltpu.CompilerParams(vmem_limit_bytes=16 << 20),
        name="project",
    )(latent, *pieces)


def per_device(queries, selection, latent_cache, value_up):
    owners, subs = lax.axis_size("ctx"), lax.axis_size("sub")
    spans, _, heads, _ = queries.shape
    chosen = jnp.transpose(selection, (0, 2, 1))
    mixed = owners <= 8

    if mixed:
        asked = [chosen] * owners
        order = sorted(range(1, owners), key=lambda e: (e == 1, e))
        for entry in order:
            asked[entry] = hop(chosen, lambda c: (c ^ entry,), ctx=owners)
        picked = pick(asked, latent_cache, spans)
        mine = [picked[0]]
        for entry in range(1, owners):
            mine.append(hop(picked[entry], lambda c: (c ^ entry,), ctx=owners))
    else:
        asked = [lax.all_gather(chosen, "ctx", axis=0, tiled=True)]
        found = pick(asked, latent_cache, spans)[0]
        mine = [lax.all_to_all(found, "ctx", split_axis=0, concat_axis=0, tiled=True)]
    other = []
    for entry, piece in enumerate(mine):
        other.append(hop(piece, lambda s: (s ^ 1,), sub=subs))
    query = jnp.transpose(queries, (0, 2, 1, 3))
    pieces, rules, query, split = weight_pieces(value_up, heads, query)
    latent = attend(chosen, query, mine, other, mixed)
    return project(latent, pieces, rules, split)


def solution(mesh):
    placed = (
        P(("groups", "ctx"), None, ("wt", "sub"), None),
        P(("groups", "ctx"), None, None),
        P(("groups", "ctx"), None, None),
        P(None, ("wt", "sub"), None),
    )

    return jax.shard_map(
        per_device,
        mesh=mesh,
        in_specs=placed,
        out_specs=P(("groups", "ctx"), None, ("wt", "sub"), None),
        check_vma=False,
    )
```

```python
import jax
import jax.numpy as jnp
from jax import lax
from jax.experimental import pallas as pl
from jax.experimental.pallas import tpu as pltpu
from jax.sharding import PartitionSpec as P

LAT = 512
ROPE = 64
NOPE = 128
SCALE = (NOPE + ROPE) ** (-0.5)
AXES = ("groups", "ctx", "wt", "sub")
PARTS = (9, 11)


SMEM = pl.BlockSpec(memory_space=pltpu.SMEM)
VMEM = pl.BlockSpec(memory_space=pltpu.VMEM)
ANY = pl.BlockSpec(memory_space=pl.ANY)
HBM = pl.BlockSpec(memory_space=pltpu.HBM)


def hop(array, move, **names):
    axes = tuple(name for name in AXES if name in names)
    sizes = [names[name] for name in axes]
    total = 1
    for size in sizes:
        total *= size
    pairs = []
    for at in range(total):
        left, place = at, []
        for size in reversed(sizes):
            place.insert(0, left % size)
            left //= size
        flat = 0
        for size, index in zip(sizes, move(*place)):
            flat = flat * size + index
        pairs.append((at, flat))
    return lax.ppermute(array, axes, pairs)


def pick(asked, cache, spans):
    parts = len(asked)
    block, width = cache.shape[1:]
    whole = asked[0].shape[0] > spans

    def kernel(*refs):
        asked_refs, cache_ref, out_refs = refs[:parts], refs[parts], refs[parts + 1 :]
        mine, slot = lax.axis_index("ctx"), lax.axis_index("sub")
        for part in range(parts):
            for first in range(0, asked[part].shape[0], spans):
                out = out_refs[0].at[first // spans] if whole else out_refs[part]
                tails = []
                for span in range(spans):
                    number = jnp.maximum(asked_refs[part][first + span, slot, mine], 0)
                    out[:, span * LAT : (span + 1) * LAT] = cache_ref[number, :, :LAT]
                    tails.append(cache_ref[number, :, LAT:])
                out[:, spans * LAT :] = jnp.concatenate(tails, axis=1)

    shape = (block, spans * width)
    if whole:
        shapes = [jax.ShapeDtypeStruct((asked[0].shape[0] // spans,) + shape, cache.dtype)]
    else:
        shapes = [jax.ShapeDtypeStruct(shape, cache.dtype)] * parts
    return pl.pallas_call(
        kernel,
        out_shape=shapes,
        in_specs=[SMEM] * parts + [VMEM],
        out_specs=[VMEM] * len(shapes),
        compiler_params=pltpu.CompilerParams(vmem_limit_bytes=16 << 20),
        name="pick",
    )(*asked, cache)


def cut(value_up, wanted):
    count = sum(len(runs) for runs in wanted)

    def kernel(whole_ref, *refs):
        outs, sems = refs[:-1], refs[-1]
        place = [lax.axis_index(name) for name in AXES]
        copies = []
        for runs, out in zip(wanted, outs):
            at = 0
            for first, heads in runs:
                copies.append(
                    pltpu.make_async_copy(
                        whole_ref.at[pl.ds(first(*place), heads)],
                        out.at[pl.ds(at, heads)],
                        sems.at[len(copies)],
                    )
                )
                at += heads
        for copy in copies:
            copy.start()
        for copy in copies:
            copy.wait()

    return pl.pallas_call(
        kernel,
        out_shape=[
            jax.ShapeDtypeStruct(
                (sum(heads for _, heads in runs),) + value_up.shape[1:], value_up.dtype
            )
            for runs in wanted
        ],
        in_specs=[HBM],
        out_specs=[VMEM] * len(wanted),
        scratch_shapes=[pltpu.SemaphoreType.DMA((count,))],
        compiler_params=pltpu.CompilerParams(vmem_limit_bytes=16 << 20),
        name="cut",
    )(pltpu.with_memory_space_constraint(value_up, pltpu.HBM))


def weight_pieces(value_up, heads, query):
    groups, ctx, wide, subs = (lax.axis_size(name) for name in AXES)
    pieces = list(cut(value_up, [[(lambda g, c, w, s: (w * subs + s) * heads, heads)]]))
    rules = [lambda g, c, w, s: [(0, w * subs + s, 0, heads)]]
    square = groups == 2 and subs == 2 and ctx % 2 == 0
    one, two = heads * PARTS[0] // 32, heads * PARTS[1] // 32
    last = 2 * one + two
    rest = heads - last
    sizes = dict(groups=groups, wt=wide, sub=subs)
    wanted, labels, moves = [], [], []

    def want(label, step, core, runs, move):
        def first_of(start):
            return lambda g, c, w, s: ((w + step) % wide * subs + core(g, s)) * heads + start(c)

        wanted.append([(first_of(start), count) for start, count in runs])
        labels.append(label)
        moves.append(move)

    for step in range(1, wide):
        if square:
            same = lambda g, w, s, step=step: (g, (w + step) % wide, s ^ g)
            cross = lambda g, w, s, step=step: (g, (w + step) % wide, s ^ g ^ 1)
            here, there = lambda g, s: s ^ g, lambda g, s: s ^ g ^ 1
            want("wone", step, here, [(lambda c: c % 2 * one, one)], same)
            want("wtwo", step, here, [(lambda c: 2 * one, two)], same)
            want("wsame", step, here, [(lambda c: last, rest)], same)
            want(
                "wcross",
                step,
                there,
                [(lambda c: (1 - c % 2) * one, one), (lambda c: last, rest)],
                cross,
            )
        else:
            for twist in range(subs):
                move = lambda g, w, s, step=step, twist=twist: (
                    g,
                    (w + step) % wide,
                    (s + twist) % subs,
                )
                there = lambda g, s, twist=twist: (s + twist) % subs
                want("wfar", step, there, [(lambda c: 0, heads)], move)
    for step in range(1, subs):
        there = lambda g, s, step=step: (s + step) % subs
        move = lambda g, w, s, step=step: (g, w, (s + step) % subs)
        want("wcore", 0, there, [(lambda c: 0, heads)], move)
    got = [None] * len(wanted)
    ahead = [at for at, label in enumerate(labels) if label == "wone"]
    for chosen in (ahead, [at for at in range(len(labels)) if at not in ahead]):
        if not chosen:
            continue
        found = cut(value_up, [wanted[at] for at in chosen])
        for at, piece in zip(chosen, found):
            got[at] = hop(piece, moves[at], **sizes)

    def add(piece, step, core, runs):
        pieces.append(piece)

        def rule(g, c, w, s):
            at, found = 0, []
            for start, count in runs:
                found.append((at, (w - step) % wide * subs + core(g, s), start(c), count))
                at += count
            return found

        rules.append(rule)

    at = 0
    for step in range(1, wide):
        if square:
            first, second, direct, crossed = got[at : at + 4]
            at += 4
            swap = lambda g: (g ^ 1,)
            side_first = hop(first, swap, groups=groups)
            over = hop(first, lambda c: (c ^ 1,), ctx=ctx)
            second, query = lax.optimization_barrier((second, query))
            side_second = hop(second, swap, groups=groups)
            here, there = lambda g, s: s ^ g, lambda g, s: s ^ g ^ 1
            own, next_to = lambda c: c % 2 * one, lambda c: (1 - c % 2) * one
            add(first, step, here, [(own, one)])
            add(over, step, here, [(next_to, one)])
            add(second, step, here, [(lambda c: 2 * one, two)])
            add(direct, step, here, [(lambda c: last, rest)])
            add(side_first, step, there, [(own, one)])
            add(side_second, step, there, [(lambda c: 2 * one, two)])
            add(crossed, step, there, [(next_to, one), (lambda c: last, rest)])
        else:
            for twist in range(subs):
                there = lambda g, s, twist=twist: (s - twist) % subs
                add(got[at], step, there, [(lambda c: 0, heads)])
                at += 1
    for step in range(1, subs):
        add(got[at], 0, lambda g, s, step=step: (s - step) % subs, [(lambda c: 0, heads)])
        at += 1
    return pieces, rules, query, 2 * one if square else 0


def attend(selection, query, mine, other, mixed):
    spans, heads, per_span, width = query.shape
    _, slots, owners = selection.shape
    block = mine[0].shape[-2]
    rotary = width - LAT
    chunks = 2
    group = heads // chunks
    landed = len(mine)

    def kernel(chosen_ref, query_ref, *refs):
        mine_refs, other_refs = refs[:landed], refs[landed : 2 * landed]
        latent, keys = refs[2 * landed :]
        at, sub = lax.axis_index("ctx"), lax.axis_index("sub")
        for span in range(spans):
            filled = jnp.int32(0)
            latent_at = slice(span * LAT, (span + 1) * LAT)
            for entry in range(owners):
                owner = at ^ entry if mixed else entry
                own = mine_refs[entry] if mixed else mine_refs[0].at[entry]
                across = other_refs[entry] if mixed else other_refs[0].at[entry]
                for slot in range(slots):
                    live = chosen_ref[span, slot, owner] >= 0
                    here = sub == slot
                    start = pl.multiple_of(jnp.minimum(filled, owners - 1) * block, block)

                    @pl.when(live)
                    def _():
                        keys[span, pl.ds(start, block), :LAT] = jnp.where(
                            here, own[:, latent_at], across[:, latent_at]
                        )
                        keys[span, pl.ds(start, block), LAT:] = jnp.where(
                            here, own[:, spans * LAT :], across[:, spans * LAT :]
                        )

                    filled = filled + live.astype(jnp.int32)
            if span:
                at_span = LAT + span * rotary
                keys[span, :, LAT:width] = keys[span, :, at_span : at_span + rotary]

        def score(step):
            span, first = step % spans, step // spans * group
            lines = query_ref[span, first : first + group].reshape(group * per_span, width)
            return lax.dot_general(
                lines,
                keys[span, :, :width],
                (((1,), (1,)), ((), ())),
                preferred_element_type=jnp.float32,
            )

        def soften(scores):
            top = jnp.max(scores, axis=1, keepdims=True)
            expo = jnp.exp((scores - top) * jnp.float32(SCALE))
            return expo.astype(jnp.bfloat16), 1.0 / jnp.sum(expo, axis=1, keepdims=True)

        def gather(step, expo, inverse):
            span, first = step % spans, step // spans * group
            mixed_rows = jnp.dot(expo, keys[span, :, :LAT], preferred_element_type=jnp.float32)
            latent[first : first + group, span] = (
                (mixed_rows * inverse).astype(jnp.bfloat16).reshape(group, per_span, LAT)
            )

        steps = chunks * spans
        scores = {step: score(step) for step in range(min(2, steps))}
        soft = {0: soften(scores.pop(0))}
        for step in range(steps):
            if step + 2 < steps:
                scores[step + 2] = score(step + 2)
            if step + 1 < steps:
                soft[step + 1] = soften(scores.pop(step + 1))
            gather(step, *soft.pop(step))

    return pl.pallas_call(
        kernel,
        out_shape=jax.ShapeDtypeStruct((heads, spans, per_span, LAT), jnp.bfloat16),
        in_specs=[SMEM] + [VMEM] * (1 + 2 * landed),
        out_specs=VMEM,
        scratch_shapes=[pltpu.VMEM((spans, owners * block, LAT + spans * rotary), jnp.bfloat16)],
        compiler_params=pltpu.CompilerParams(vmem_limit_bytes=(16 if mixed else 44) << 20),
        name="attend",
    )(selection, query, *mine, *other)


def project(latent, pieces, rules, split):
    heads, spans, per_span, _ = latent.shape
    rows, values = pieces[0].shape[1:]
    tokens = spans * per_span
    parts = len(pieces)
    pitch = heads + 8

    def kernel(latent_ref, *refs):
        piece_refs = refs[:parts]
        out_ref, weights, summed, result, weight_sems, out_sem = refs[parts:]
        place = [lax.axis_index(name) for name in AXES]
        arrivals = [[], []]

        def bring(group, piece, head_from, number, head_to, count):
            row_at = pl.multiple_of(number * rows, rows)
            arrivals[group].append(
                pltpu.make_async_copy(
                    piece.at[pl.ds(head_from, count)],
                    weights.at[pl.ds(head_to, count), pl.ds(row_at, rows)],
                    weight_sems.at[group],
                )
            )

        for piece, rule in zip(piece_refs, rules):
            for head_from, number, head_to, count in rule(*place):
                if not isinstance(head_to, int) or head_to + count <= split:
                    bring(1, piece, head_from, number, head_to, count)
                elif head_to >= split:
                    bring(0, piece, head_from, number, head_to, count)
                else:
                    low = split - head_to
                    bring(0, piece, head_from + low, number, split, count - low)
                    bring(1, piece, head_from, number, head_to, low)
        for group in arrivals:
            for copy in group:
                copy.start()

        departures = []
        done = set()
        for position, head in enumerate(list(range(split, heads)) + list(range(split - 1, -1, -1))):
            if position in (0, heads - split):
                for copy in arrivals[0 if position == 0 and split < heads else 1]:
                    copy.wait()
            summed[pl.ds(head, tokens, stride=pitch), :] = jnp.dot(
                latent_ref[head].reshape(tokens, LAT),
                weights[head],
                preferred_element_type=jnp.float32,
            )
            done.add(head)
            first = head // 16 * 16
            if not done.issuperset(range(first, first + 16)):
                continue
            for token in range(tokens):
                line = summed[token * pitch + first : token * pitch + first + 16, :]
                result[token // per_span, token % per_span, first : first + 16] = line.astype(
                    jnp.bfloat16
                )
            departures.append(
                pltpu.make_async_copy(
                    result.at[:, :, pl.ds(first, 16)], out_ref.at[:, :, pl.ds(first, 16)], out_sem
                )
            )
            departures[-1].start()
        for copy in departures:
            copy.wait()

    return pl.pallas_call(
        kernel,
        out_shape=jax.ShapeDtypeStruct((spans, per_span, heads, values), jnp.bfloat16),
        in_specs=[VMEM] + [ANY] * parts,
        out_specs=ANY,
        scratch_shapes=[
            pltpu.VMEM((heads, LAT, values), jnp.bfloat16),
            pltpu.VMEM((tokens * pitch, values), jnp.float32),
            pltpu.VMEM((spans, per_span, heads, values), jnp.bfloat16),
            pltpu.SemaphoreType.DMA((2,)),
            pltpu.SemaphoreType.DMA,
        ],
        compiler_params=pltpu.CompilerParams(vmem_limit_bytes=16 << 20),
        name="project",
    )(latent, *pieces)


def per_device(queries, selection, latent_cache, value_up):
    owners, subs = lax.axis_size("ctx"), lax.axis_size("sub")
    spans, _, heads, _ = queries.shape
    chosen = jnp.transpose(selection, (0, 2, 1))
    mixed = owners <= 8

    if mixed:
        asked = [chosen] * owners
        order = sorted(range(1, owners), key=lambda e: (e == 1, e))
        for entry in order:
            asked[entry] = hop(chosen, lambda c: (c ^ entry,), ctx=owners)
        picked = pick(asked, latent_cache, spans)
        mine = [picked[0]]
        for entry in range(1, owners):
            mine.append(hop(picked[entry], lambda c: (c ^ entry,), ctx=owners))
    else:
        asked = [lax.all_gather(chosen, "ctx", axis=0, tiled=True)]
        found = pick(asked, latent_cache, spans)[0]
        mine = [lax.all_to_all(found, "ctx", split_axis=0, concat_axis=0, tiled=True)]
    other = []
    for entry, piece in enumerate(mine):
        other.append(hop(piece, lambda s: (s ^ 1,), sub=subs))
    query = jnp.transpose(queries, (0, 2, 1, 3))
    pieces, rules, query, split = weight_pieces(value_up, heads, query)
    latent = attend(chosen, query, mine, other, mixed)
    return project(latent, pieces, rules, split)


def solution(mesh):
    placed = (
        P(("groups", "ctx"), None, ("wt", "sub"), None),
        P(("groups", "ctx"), None, None),
        P(("groups", "ctx"), None, None),
        P(None, ("wt", "sub"), None),
    )

    return jax.shard_map(
        per_device,
        mesh=mesh,
        in_specs=placed,
        out_specs=P(("groups", "ctx"), None, ("wt", "sub"), None),
        check_vma=False,
    )
```
